32 devices in a mesh: groups: 2 (over y), section: 4 (over z), replica: 2 (over x), tensor: 2 (over core).
Axes of the slice: x: 2, y: 2, z: 4, core: 2. Of those that a mesh axis runs over, the one named last changes fastest.
Arguments:
- inflow: bfloat16 [4, 1024, 1152], P('section', ('groups', 'replica')), parts along dimension 1, may hold values from -6 to 6
- fresh_rows: bfloat16 [2, 4, 256, 1152], P(None, ('groups', 'replica'), 'section'), parts along dimension 1, may hold values from -6 to 6
- lin_weight: bfloat16 [4, 1152, 1152], P('section', None, 'tensor'), may hold values from -0.125 to 0.125
- qkv_weight: bfloat16 [4, 3, 1152, 576], P('section', None, None, 'tensor'), may hold values from -2 to 2
- out_weight: bfloat16 [4, 576, 1152], P('section', 'tensor'), may hold values from -0.25 to 0.25
- mod_weight: bfloat16 [4, 128, 2, 1152], P('section', None, None, 'tensor'), may hold values from -0.5 to 0.5
- plan: int32 [3, 4], P(None, 'section'), may hold values from 0 to 5
- timesteps: int32 [6, 4], P(None, ('groups', 'replica')), parts along dimension 1, may hold values from 0 to 999
Outputs:
- settled: float32 [4, 1024, 1152], P('section', ('groups', 'replica'), 'tensor'), parts along dimension 1
The draws below stay inside these ranges and needn't reach their ends.
There are 2 independent parts, one for each index of `groups`. The reference program is written for one: setup_inputs(seed, part) draws one part's arguments, and reference() takes and returns one part's arrays. A program takes and returns all parts, laid end to end along the dimension named above; an argument that names none is the same for every part. Nothing has to cross between parts.
All inputs are finite; a program needn't handle non-finite values.
Results may differ from the reference program's by a relative error of at most 0.039.
Values may be sent and summed in bfloat16 or wider, within the bound.
No kernel may reach another device: no remote copies, remote signals or barrier semaphores. Data moves between devices by JAX's collectives and lax.ppermute only.
A program may use at most 64 MiB of HBM per device.

```python
import math
import jax
import jax.numpy as jnp
from jax import lax

D = 1152
DH = 72
HEADS = 8
HD = 576
FREQ = 128
NT = 1000
TOKS = 256
TICKS = 3
IMAGES = 2
ROWS = 512
SECTIONS = 4
MICRO = 6
N_TENSOR = 2


def draw_qkv_weight(key, part):
    key_list = jax.random.split(key, 1)
    shaped = jax.random.normal(key_list[0], (SECTIONS, 3, D, HD), jnp.float32) * (1.0 / math.sqrt(D))
    return jnp.clip(shaped, -2.0, 2.0).astype(jnp.bfloat16)


def touch_ends(entries, rng, smallest, largest):
    longest = entries.shape.index(max(entries.shape))
    spots = []
    for shift in (0, 1):
        where = [jax.random.randint(jax.random.fold_in(rng, axis), (), 0, length) for axis, length in enumerate(entries.shape)]
        where[longest] = (where[longest] + shift) % entries.shape[longest]
        spots.append(tuple(where))
    return entries.at[spots[0]].set(smallest).at[spots[1]].set(largest)


def level_of(own_key, extent, cuts, least, high):
    def one(dim, parts):
        steps = jax.random.uniform(jax.random.fold_in(jax.random.fold_in(own_key, 6), dim), (parts,), jnp.float32, least / len(cuts), high / len(cuts))
        return jnp.repeat(jnp.exp(steps), extent[dim] // parts).reshape((-1,) + (1,) * (len(extent) - dim - 1))

    factor_of = one(*cuts[0])
    for cut in cuts[1:]:
        factor_of = factor_of * one(*cut)
    return factor_of


def normal_values(key, shape, deviation, reach, cuts=(), held_as=jnp.bfloat16):
    values = deviation * jax.random.normal(key, shape, jnp.float32)
    if cuts:
        values = values * level_of(key, shape, cuts, -0.22, 0.18)
    return jnp.clip(values, -reach, reach).astype(held_as)


def setup_inputs(seed: int = 0, part: int = 0) -> dict:
    arg_keys = jax.random.split(jax.random.key(seed), 9)
    part_keys = jax.random.split(jax.random.fold_in(arg_keys[8], part), 9)
    return {
        "inflow": normal_values(part_keys[0], (SECTIONS, ROWS, D), 1.0, 6.0, ((0, 4), (1, 2))),
        "fresh_rows": normal_values(part_keys[1], (TICKS - 1, IMAGES, TOKS, D), 1.0, 6.0, ((1, 2), (2, 4))),
        "lin_weight": normal_values(arg_keys[2], (SECTIONS, D, D), (2 * D) ** -0.5, 0.125, ((0, 4), (2, 2))),
        "qkv_weight": draw_qkv_weight(jax.random.fold_in(arg_keys[8], 71), part),
        "out_weight": normal_values(arg_keys[4], (SECTIONS, HD, D), HD ** -0.5, 0.25, ((0, 4), (1, 2))),
        "mod_weight": normal_values(arg_keys[5], (SECTIONS, FREQ, 2, D), FREQ ** -0.5, 0.5, ((0, 4), (3, 2))),
        "plan": touch_ends(jax.random.randint(arg_keys[6], (TICKS, SECTIONS), 0, MICRO), jax.random.fold_in(arg_keys[6], 1), 0, MICRO - 1).astype(jnp.int32),
        "timesteps": touch_ends(jax.random.randint(part_keys[7], (MICRO, IMAGES), 0, NT), jax.random.fold_in(part_keys[7], 1), 0, NT - 1).astype(jnp.int32),
    }


epsilon = 1e-06

def timestep_embed(times):
    half_width = FREQ // 2
    frequency = jnp.exp(-math.log(10000.0) * jnp.arange(half_width, dtype=jnp.float32) / half_width)
    phases = times.astype(jnp.float32)[:, None] * frequency[None, :]
    return jnp.concatenate([jnp.cos(phases), jnp.sin(phases)], axis=1)

def attention_block(arrays):
    hidden, modulation, weights_qkv, weights_out = arrays
    image_count = modulation.shape[0]
    widths = hidden.shape[1]
    values_f = hidden.reshape(image_count, TOKS, widths)
    centred = values_f - lax.optimization_barrier(jnp.mean(values_f, axis=-1, keepdims=True))
    variance = lax.optimization_barrier(jnp.mean(centred * centred, axis=-1, keepdims=True))
    normed = centred * lax.rsqrt(variance + epsilon)
    scaling = modulation[:, 0].astype(jnp.float32)[:, None, :]
    gating = modulation[:, 1].astype(jnp.float32)[:, None, :]
    mixed = (normed * (1.0 + scaling)).astype(jnp.bfloat16).reshape(-1, widths)
    projected = [jnp.dot(mixed, weights_qkv[index], preferred_element_type=jnp.float32).astype(jnp.bfloat16).reshape(image_count, TOKS, HEADS, DH) for index in range(3)]
    scores = jnp.einsum('iqhe,ikhe->ihqk', projected[0].astype(jnp.float32), projected[1].astype(jnp.float32)) * (1.0 / math.sqrt(DH))
    weights_soft = jax.nn.softmax(scores, axis=-1).astype(jnp.bfloat16)
    attended = jnp.einsum('ihqk,ikhe->iqhe', weights_soft.astype(jnp.float32), projected[2].astype(jnp.float32)).astype(jnp.bfloat16).reshape(-1, HEADS * DH)
    group_cols = HEADS * DH // N_TENSOR
    summed = jnp.zeros((attended.shape[0], widths), jnp.float32)
    for group in range(N_TENSOR):
        lower = group * group_cols
        piece = jnp.dot(attended[:, lower:lower + group_cols], weights_out[lower:lower + group_cols], preferred_element_type=jnp.float32)
        summed = summed + lax.optimization_barrier(piece.astype(jnp.bfloat16)).astype(jnp.float32)
    result = values_f + gating * summed.reshape(image_count, TOKS, widths)
    return result.reshape(-1, widths)

def section_product(couple):
    return jnp.dot(couple[0].astype(jnp.bfloat16), couple[1], preferred_element_type=jnp.float32)

def reference(inflow, fresh_rows, lin_weight, qkv_weight, out_weight, mod_weight, plan, timesteps):
    section_count = inflow.shape[0]
    upper = (jnp.arange(section_count) >= section_count // 2)[:, None, None]
    current = inflow.astype(jnp.float32)
    settled = current
    for tick_index in range(TICKS):
        products = lax.map(section_product, (current, lin_weight))
        skipped = products[::-1]
        hidden = jnp.where(upper, products + skipped, current)
        times = timesteps[plan[tick_index]]
        embedded = timestep_embed(times.reshape(-1)).reshape(section_count, -1, FREQ)
        modulation = jnp.einsum('sif,sfcd->sicd', embedded, mod_weight.astype(jnp.float32), precision=lax.Precision.HIGHEST).astype(jnp.bfloat16)
        settled = lax.map(attention_block, (hidden, modulation, qkv_weight, out_weight))
        if tick_index + 1 < TICKS:
            arriving = fresh_rows[tick_index].astype(jnp.float32).reshape(1, -1, settled.shape[2])
            current = jnp.concatenate([arriving, settled[:-1]], axis=0)
    return settled
```

```python
import functools
import math

import jax
import jax.numpy as jnp
from jax import lax
from jax.experimental import pallas as pl
from jax.experimental.pallas import tpu as pltpu
from jax.sharding import PartitionSpec as P

DH = 72
FREQ = 128
TICKS = 3
EPSILON = 1e-06


VMEM = pl.BlockSpec(memory_space=pltpu.VMEM)
SMEM = pl.BlockSpec(memory_space=pltpu.SMEM)


def call(body, outs, in_specs, flops, args, name, scratch=()):
    moved = sum(math.prod(a.shape) * a.dtype.itemsize for a in (*args, *outs))
    return pl.pallas_call(
        body,
        out_shape=tuple(outs),
        in_specs=in_specs,
        out_specs=tuple(VMEM for _ in outs),
        scratch_shapes=list(scratch),
        compiler_params=pltpu.CompilerParams(vmem_limit_bytes=24 << 20),
        cost_estimate=pl.CostEstimate(flops=flops, bytes_accessed=moved, transcendentals=0),
        name=name,
    )(*args)


def like(shape, dtype):
    return jax.ShapeDtypeStruct(shape, dtype)


def halves(tensor_index, half):
    own = pl.ds(pl.multiple_of(tensor_index * half, 16), half)
    other = pl.ds(pl.multiple_of((1 - tensor_index) * half, 16), half)
    return own, other


def modulation_kernel(where, plan, times, own_ref, other_ref, *outs):
    half_freq = FREQ // 2
    lanes = 128
    group = lanes // 4
    position = lax.broadcasted_iota(jnp.int32, (half_freq, lanes), 0).astype(jnp.float32)
    lane = lax.broadcasted_iota(jnp.int32, (half_freq, lanes), 1)
    frequency = jnp.exp(-math.log(10000.0) * position / half_freq)
    stamp = jnp.zeros((half_freq, lanes), jnp.float32)
    for tick in range(TICKS):
        moment = times[plan[tick, 0], 0].astype(jnp.float32)
        stamp = jnp.where(lane // group == tick, moment, stamp)
    phases = stamp * frequency
    embedded = jnp.concatenate([jnp.cos(phases), jnp.sin(phases)], axis=0)
    parts = []
    rest = embedded
    for _ in range(3):
        part = rest.astype(jnp.bfloat16).astype(jnp.float32)
        parts.append(part)
        rest = rest - part
    stacked = jnp.concatenate(parts, axis=0)
    spread = jnp.concatenate(
        [
            jnp.broadcast_to(stacked[:, tick * group : tick * group + 1], (3 * FREQ, lanes))
            for tick in range(TICKS)
        ],
        axis=1,
    ).astype(jnp.bfloat16)
    half = own_ref.shape[1]
    for ref, rows in zip((own_ref, other_ref), halves(where[0], half)):
        for kind in range(2):
            weight = ref[kind]
            product = jnp.dot(
                jnp.concatenate([weight] * 3, axis=1), spread, preferred_element_type=jnp.float32
            ).astype(jnp.bfloat16)
            for tick in range(TICKS):
                outs[kind * TICKS + tick][rows, :] = product[:, tick * lanes : (tick + 1) * lanes]


def normalised(hidden, scale):
    count = hidden.shape[0]
    centred = hidden - jnp.sum(hidden, axis=0, keepdims=True) * (1.0 / count)
    variance = jnp.sum(centred * centred, axis=0, keepdims=True) * (1.0 / count)
    normed = centred * lax.rsqrt(variance + EPSILON)
    return (normed * (1.0 + scale.astype(jnp.float32))).astype(jnp.bfloat16)


def first_norm_kernel(where, x_ref, scale_ref, own_ref, other_ref, hidden_ref):
    tokens = own_ref.shape[1]
    for index in range(2):
        hidden = x_ref[:, index * tokens : (index + 1) * tokens].astype(jnp.float32)
        mixed = normalised(hidden, scale_ref[...])

        @pl.when(where[0] == index)
        def _():
            own_ref[...] = mixed
            hidden_ref[...] = hidden.astype(jnp.bfloat16)

        @pl.when(where[0] != index)
        def _():
            other_ref[...] = mixed


def norm_kernel(x_ref, scale_ref, mixed_ref):
    mixed_ref[...] = normalised(x_ref[...].astype(jnp.float32), scale_ref[...])


def product_kernel(where, x_ref, own_ref, other_ref, wide_ref, narrow_ref):
    half = own_ref.shape[0]
    for ref, rows in zip((own_ref, other_ref), halves(where[0], half)):
        product = jnp.dot(ref[...], x_ref[...], preferred_element_type=jnp.float32)
        wide_ref[rows, :] = product
        narrow_ref[rows, :] = product.astype(jnp.bfloat16)


def joined_kernel(where, x_ref, product_ref, skip_ref, scale_ref, mixed_ref, hidden_ref):
    @pl.when(where[1] == 1)
    def _():
        hidden = product_ref[...] + skip_ref[...].astype(jnp.float32)
        hidden_ref[...] = hidden
        mixed_ref[...] = normalised(hidden, scale_ref[...])

    @pl.when(where[1] == 0)
    def _():
        hidden = x_ref[...].astype(jnp.float32)
        hidden_ref[...] = hidden
        mixed_ref[...] = normalised(hidden, scale_ref[...])


def block_kernel(last, where, own_ref, other_ref, hidden_ref, gate_ref, qkv_own, qkv_other, out_own, out_other, *results):
    own = own_ref[...]
    both = jnp.concatenate([own, other_ref[...]], axis=1)
    head_cols = qkv_own.shape[1]
    total = None
    for qkv_ref, out_ref in ((qkv_own, out_own), (qkv_other, out_other)):
        query = jnp.dot(qkv_ref[0], own, preferred_element_type=jnp.float32).astype(jnp.bfloat16)
        key = jnp.dot(qkv_ref[1], both, preferred_element_type=jnp.float32).astype(jnp.bfloat16)
        value = jnp.dot(qkv_ref[2], both, preferred_element_type=jnp.float32).astype(jnp.bfloat16)
        pieces = []
        for start in range(0, head_cols, DH):
            rows = slice(start, start + DH)
            scores = lax.dot_general(
                key[rows], query[rows], (((0,), (0,)), ((), ())), preferred_element_type=jnp.float32
            ) * (1.0 / math.sqrt(DH))
            raised = jnp.exp(scores - jnp.max(scores, axis=0, keepdims=True))
            weight = jnp.sum(raised, axis=0, keepdims=True)
            attended = jnp.dot(value[rows], raised.astype(jnp.bfloat16), preferred_element_type=jnp.float32)
            pieces.append(attended / weight)
        heads = jnp.concatenate(pieces, axis=0).astype(jnp.bfloat16)
        term = jnp.dot(out_ref[...], heads, preferred_element_type=jnp.float32)
        term = term.astype(jnp.bfloat16).astype(jnp.float32)
        total = term if total is None else total + term
    result = hidden_ref[...].astype(jnp.float32) + gate_ref[...].astype(jnp.float32) * total
    if last:
        kept_ref, sent_ref, full_ref = results
        full_ref[...] = result
        own_rows, other_rows = halves(where[0], kept_ref.shape[0])
        kept_ref[...] = full_ref[own_rows, :]
        sent_ref[...] = full_ref[other_rows, :]
    else:
        results[0][...] = result.astype(jnp.bfloat16)


def on_device(inflow, fresh_rows, lin_weight, qkv_weight, out_weight, mod_weight, plan, timesteps):
    sections = lax.axis_size("section")
    middle = sections // 2
    section = lax.axis_index("section")
    core = lax.axis_index("tensor")
    upper = section >= middle
    _, row_count, width = inflow.shape
    tokens = row_count // lax.axis_size("tensor")
    half = lin_weight.shape[2]
    head_cols = out_weight.shape[1]
    if lax.axis_size("tensor") != 2 or timesteps.shape[1] != 1:
        raise ValueError("unsupported split")
    where = jnp.stack([core, upper.astype(jnp.int32)]).astype(jnp.int32)

    def swapped(value, name):
        with jax.named_scope(name):
            return lax.ppermute(value, "tensor", [(0, 1), (1, 0)])

    def moved(value, pairs, name):
        with jax.named_scope(name):
            return lax.ppermute(value, "section", pairs)

    mirrors = [(low, sections - 1 - low) for low in range(middle)]
    lower_pairs = [(low, low + 1) for low in range(middle - 1)]
    upper_pairs = [(low, low + 1) for low in range(middle - 1, sections - 1)]

    mod_own = jnp.transpose(mod_weight[0], (1, 2, 0))
    qkv_own = jnp.transpose(qkv_weight[0], (0, 2, 1))
    lin_own = jnp.transpose(lin_weight[0], (1, 0))
    out_own = jnp.transpose(out_weight[0], (1, 0))
    mod_other = swapped(mod_own, "swap_mod")
    qkv_other = swapped(qkv_own, "swap_qkv")
    out_other = swapped(out_own, "swap_out")
    lin_other = swapped(lin_own, "swap_lin")
    first = jnp.transpose(inflow[0], (1, 0))

    block = fresh_rows[:, 0]
    step = 1
    while step < middle:
        pairs = [
            ((low + step) * 2 + side, low * 2 + side)
            for side in range(2)
            for low in range(side * middle, (side + 1) * middle, 2 * step)
        ]
        with jax.named_scope("fresh_tree"):
            received = lax.ppermute(block, ("section", "tensor"), pairs)
        block = jnp.concatenate([block, received], axis=1)
        step *= 2
    with jax.named_scope("fresh_hop"):
        crossed = lax.ppermute(block, ("section", "tensor"), [(middle * 2 + 1, 1)])
    fresh = jnp.transpose(jnp.where(core == 1, crossed, block), (0, 2, 1))

    narrow = like((width, tokens), jnp.bfloat16)
    wide = like((width, tokens), jnp.float32)
    product_flops = 2 * width * width * tokens
    block_flops = 6 * product_flops

    modulations = call(
        modulation_kernel,
        [like((width, 128), jnp.bfloat16)] * (2 * TICKS),
        [SMEM, SMEM, SMEM, VMEM, VMEM],
        2 * 2 * width * 3 * FREQ * 3 * 128,
        (where, plan, timesteps, mod_own, mod_other),
        "modulation",
    )
    scales, gates = modulations[:TICKS], modulations[TICKS:]

    def norm(value, tick):
        return call(norm_kernel, [narrow], [VMEM] * 2, 10 * width * tokens, (value, scales[tick]), "norm")[0]

    def product(value):
        return call(
            product_kernel, [wide, narrow], [SMEM] + [VMEM] * 3, product_flops,
            (where, value, lin_own, lin_other), "product",
        )

    def joined(value, products, skip, tick):
        return call(
            joined_kernel, [narrow, wide], [SMEM] + [VMEM] * 4, 12 * width * tokens,
            (where, value, products, skip, scales[tick]), "joined",
        )

    def attention(own, other, hidden, tick, last=False):
        if last:
            outs = [like((half, tokens), jnp.float32)] * 2
            scratch = [pltpu.VMEM((width, tokens), jnp.float32)]
        else:
            outs = [narrow]
            scratch = []
        return call(
            functools.partial(block_kernel, last), outs, [SMEM] + [VMEM] * 8, block_flops,
            (where, own, other, hidden, gates[tick], qkv_own, qkv_other, out_own, out_other),
            "attention_last" if last else "attention", scratch,
        )

    own, other, hidden = call(
        first_norm_kernel, [narrow, narrow, narrow], [SMEM, VMEM, VMEM], 20 * width * tokens,
        (where, first, scales[0]), "first_norm",
    )
    if middle <= sections - TICKS:
        products, outgoing = product(hidden)
        skip = moved(outgoing, mirrors, "mirror0")
        own, hidden = joined(hidden, products, skip, 0)
        other = swapped(own, "swap0")
    settled = attention(own, other, hidden, 0)[0]

    arrived = moved(settled, [(low, low + 1) for low in range(sections - 1)], "relay0")
    current = jnp.where(section == 0, fresh[0], arrived)
    own = norm(current, 1)
    other = swapped(own, "swap1")
    products, outgoing = product(current)
    skip = moved(outgoing, mirrors, "mirror1")
    down = attention(own, other, current, 1)[0]
    if lower_pairs:
        arrived_low = moved(down, lower_pairs, "relay1_low")
        current_low = jnp.where(section == 0, fresh[1], arrived_low)
    else:
        current_low = fresh[1]
    own, hidden = joined(current, products, skip, 1)
    other = swapped(own, "swap2")
    up = attention(own, other, hidden, 1)[0]

    arrived = moved(jnp.where(upper, up, down), upper_pairs, "relay1_up")
    _, outgoing = product(current_low)
    skip = moved(outgoing, mirrors, "mirror2")
    products, _ = product(arrived)
    own, hidden = joined(current_low, products, skip, 2)
    other = swapped(own, "swap3")
    kept, sent = attention(own, other, hidden, 2, last=True)
    received = swapped(sent, "swap_out_columns")
    columns = jnp.where(
        core == 0,
        jnp.concatenate([kept, received], axis=1),
        jnp.concatenate([received, kept], axis=1),
    )
    return jnp.transpose(columns, (1, 0))[None]


def solution(mesh):
    return jax.shard_map(
        on_device,
        mesh=mesh,
        in_specs=(
            P("section", ("groups", "replica"), None),
            P(None, ("groups", "replica"), "section", None),
            P("section", None, "tensor"),
            P("section", None, None, "tensor"),
            P("section", "tensor", None),
            P("section", None, None, "tensor"),
            P(None, "section"),
            P(None, ("groups", "replica")),
        ),
        out_specs=P("section", ("groups", "replica"), "tensor"),
        check_vma=False,
    )
```

```python
import functools
import math

import jax
import jax.numpy as jnp
from jax import lax
from jax.experimental import pallas as pl
from jax.experimental.pallas import tpu as pltpu
from jax.sharding import PartitionSpec as P

DH = 72
FREQ = 128
TICKS = 3
EPSILON = 1e-06


VMEM = pl.BlockSpec(memory_space=pltpu.VMEM)
SMEM = pl.BlockSpec(memory_space=pltpu.SMEM)
ANY = pl.BlockSpec(memory_space=pl.ANY)
TICK_LANES = 32


def call(body, outs, in_specs, flops, args, name, scratch=()):
    moved = sum(math.prod(a.shape) * a.dtype.itemsize for a in (*args, *outs))
    return pl.pallas_call(
        body,
        out_shape=tuple(outs),
        in_specs=in_specs,
        out_specs=tuple(VMEM for _ in outs),
        scratch_shapes=list(scratch),
        compiler_params=pltpu.CompilerParams(vmem_limit_bytes=24 << 20),
        cost_estimate=pl.CostEstimate(flops=flops, bytes_accessed=moved, transcendentals=0),
        name=name,
    )(*args)


def like(shape, dtype):
    return jax.ShapeDtypeStruct(shape, dtype)


def halves(tensor_index, half):
    own = pl.ds(pl.multiple_of(tensor_index * half, 16), half)
    other = pl.ds(pl.multiple_of((1 - tensor_index) * half, 16), half)
    return own, other


def normalised(hidden, scale):
    count = hidden.shape[0]
    centred = hidden - jnp.sum(hidden, axis=0, keepdims=True) * (1.0 / count)
    variance = jnp.sum(centred * centred, axis=0, keepdims=True) * (1.0 / count)
    normed = centred * lax.rsqrt(variance + EPSILON)
    return (normed * (1.0 + scale)).astype(jnp.bfloat16)


def column(ref, tick):
    lane = tick * TICK_LANES
    return ref[:, lane : lane + 1].astype(jnp.float32)


def first_kernel(where, plan, times, mod_own, mod_other, x_ref, scale_ref, gate_ref, own_ref, other_ref, hidden_ref):
    half_freq = FREQ // 2
    lanes = scale_ref.shape[1]
    position = lax.broadcasted_iota(jnp.int32, (half_freq, lanes), 0).astype(jnp.float32)
    lane = lax.broadcasted_iota(jnp.int32, (half_freq, lanes), 1)
    frequency = jnp.exp(-math.log(10000.0) * position / half_freq)
    stamp = jnp.zeros((half_freq, lanes), jnp.float32)
    for tick in range(TICKS):
        moment = times[plan[tick, 0], 0].astype(jnp.float32)
        stamp = jnp.where(lane // TICK_LANES == tick, moment, stamp)
    phases = stamp * frequency
    rest = jnp.concatenate([jnp.cos(phases), jnp.sin(phases)], axis=0)
    parts = []
    for _ in range(3):
        part = rest.astype(jnp.bfloat16)
        parts.append(part)
        rest = rest - part.astype(jnp.float32)
    stacked = jnp.concatenate(parts, axis=0)
    half = mod_own.shape[1]
    for ref, rows in zip((mod_own, mod_other), halves(where[0], half)):
        for kind, target in enumerate((scale_ref, gate_ref)):
            weight = jnp.concatenate([ref[kind]] * 3, axis=1)
            product = jnp.dot(weight, stacked, preferred_element_type=jnp.float32)
            target[rows, :] = product.astype(jnp.bfloat16)
    tokens = own_ref.shape[1]
    scale = column(scale_ref, 0)
    for index in range(2):
        rows = x_ref[index * tokens : (index + 1) * tokens, :]
        hidden = jnp.transpose(rows.astype(jnp.float32), (1, 0))
        mixed = normalised(hidden, scale)

        @pl.when(where[0] == index)
        def _():
            own_ref[...] = mixed
            hidden_ref[...] = hidden.astype(jnp.bfloat16)

        @pl.when(where[0] != index)
        def _():
            other_ref[...] = mixed


def fresh_kernel(where, *refs):
    *blocks, result_ref = refs
    tokens = blocks[0].shape[1]

    @pl.when(where[2] == 0)
    def _():
        for tick in range(result_ref.shape[0]):
            head = jnp.where(where[0] == 0, blocks[0][tick].astype(jnp.float32), blocks[1][tick].astype(jnp.float32))
            rows = [head] + [ref[tick].astype(jnp.float32) for ref in blocks[2:]]
            result_ref[tick] = jnp.transpose(jnp.concatenate(rows, axis=0), (1, 0)).astype(jnp.bfloat16)


def norm_kernel(tick, where, arrived_ref, fresh_ref, scale_ref, current_ref, mixed_ref):
    def put(value):
        current_ref[...] = value
        mixed_ref[...] = normalised(value.astype(jnp.float32), column(scale_ref, tick))

    @pl.when(where[2] == 0)
    def _():
        put(fresh_ref[tick - 1])

    @pl.when(where[2] != 0)
    def _():
        put(arrived_ref[...])


def product_kernel(where, x_ref, own_ref, other_ref, wide_ref, narrow_ref):
    half = own_ref.shape[0]
    for ref, rows in zip((own_ref, other_ref), halves(where[0], half)):
        product = jnp.dot(ref[...], x_ref[...], preferred_element_type=jnp.float32)
        wide_ref[rows, :] = product
        narrow_ref[rows, :] = product.astype(jnp.bfloat16)


def skip_kernel(tick, where, arrived_ref, fresh_ref, own_ref, other_ref, order_ref, current_ref, narrow_ref):
    half = own_ref.shape[0]

    @pl.when(where[2] == 0)
    def _():
        current_ref[...] = fresh_ref[tick - 1]

    @pl.when(where[2] != 0)
    def _():
        current_ref[...] = arrived_ref[...]

    for ref, rows in zip((own_ref, other_ref), halves(where[0], half)):
        product = jnp.dot(ref[...], current_ref[...], preferred_element_type=jnp.float32)
        narrow_ref[rows, :] = product.astype(jnp.bfloat16)


def joined_kernel(tick, where, x_ref, product_ref, skip_ref, scale_ref, order_ref, mixed_ref, hidden_ref):
    @pl.when(where[1] == 1)
    def _():
        hidden_ref[...] = product_ref[...] + skip_ref[...].astype(jnp.float32)

    @pl.when(where[1] == 0)
    def _():
        hidden_ref[...] = x_ref[...].astype(jnp.float32)

    mixed_ref[...] = normalised(hidden_ref[...], column(scale_ref, tick))


def block_kernel(tick, stage, where, own_ref, other_ref, hidden_ref, gate_ref, qkv_own, qkv_other, out_own, out_other, *results):
    own = own_ref[...]
    both = jnp.concatenate([own, other_ref[...]], axis=1)
    head_cols = qkv_own.shape[1]
    if stage == "first":
        turned = results[1:]
        for source, target in zip((out_own, out_other), turned):
            target[...] = jnp.transpose(source[...].astype(jnp.float32), (1, 0)).astype(jnp.bfloat16)
    else:
        turned = (out_own, out_other)
    total = None
    for qkv_ref, out_ref in zip((qkv_own, qkv_other), turned):
        query = jnp.dot(qkv_ref[0], own, preferred_element_type=jnp.float32).astype(jnp.bfloat16)
        key = jnp.dot(qkv_ref[1], both, preferred_element_type=jnp.float32).astype(jnp.bfloat16)
        value = jnp.dot(qkv_ref[2], both, preferred_element_type=jnp.float32).astype(jnp.bfloat16)
        pieces = []
        for start in range(0, head_cols, DH):
            rows = slice(start, start + DH)
            scores = lax.dot_general(
                key[rows], query[rows], (((0,), (0,)), ((), ())), preferred_element_type=jnp.float32
            ) * (1.0 / math.sqrt(DH))
            raised = jnp.exp(scores - jnp.max(scores, axis=0, keepdims=True))
            weight = jnp.sum(raised, axis=0, keepdims=True)
            attended = jnp.dot(value[rows], raised.astype(jnp.bfloat16), preferred_element_type=jnp.float32)
            pieces.append(attended / weight)
        heads = jnp.concatenate(pieces, axis=0).astype(jnp.bfloat16)
        term = jnp.dot(out_ref[...], heads, preferred_element_type=jnp.float32)
        term = term.astype(jnp.bfloat16).astype(jnp.float32)
        total = term if total is None else total + term
    result = hidden_ref[...].astype(jnp.float32) + column(gate_ref, tick) * total
    if stage == "last":
        kept_ref, sent_ref, full_ref = results
        full_ref[...] = result
        own_rows, other_rows = halves(where[0], kept_ref.shape[0])
        kept_ref[...] = full_ref[own_rows, :]
        sent_ref[...] = full_ref[other_rows, :]
    else:
        results[0][...] = result.astype(jnp.bfloat16)


def on_device(inflow, fresh_rows, lin_weight, qkv_weight, out_weight, mod_weight, plan, timesteps):
    sections = lax.axis_size("section")
    middle = sections // 2
    section = lax.axis_index("section")
    core = lax.axis_index("tensor")
    _, row_count, width = inflow.shape
    tokens = row_count // lax.axis_size("tensor")
    half = lin_weight.shape[2]
    head_cols = out_weight.shape[1]
    if lax.axis_size("tensor") != 2 or timesteps.shape[1] != 1:
        raise ValueError("unsupported split")
    where = jnp.stack([core, (section >= middle).astype(jnp.int32), section]).astype(jnp.int32)

    def swapped(value, name):
        with jax.named_scope(name):
            return lax.ppermute(value, "tensor", [(0, 1), (1, 0)])

    def moved(value, pairs, name):
        with jax.named_scope(name):
            return lax.ppermute(value, "section", pairs)

    mod_own = jnp.transpose(mod_weight[0], (1, 2, 0))
    qkv_own = jnp.transpose(qkv_weight[0], (0, 2, 1))
    lin_own = jnp.transpose(lin_weight[0], (1, 0))
    out_own = out_weight[0]
    mod_other = swapped(mod_own, "swap_mod")
    qkv_other = swapped(qkv_own, "swap_qkv")
    out_other = swapped(out_own, "swap_out")
    lin_other = swapped(lin_own, "swap_lin")

    blocks = [fresh_rows[:, 0]]
    for place in range(middle):
        pairs = [
            ((side * middle + place) * 2 + side, side) for side in range(2) if side or place
        ]
        with jax.named_scope("fresh"):
            blocks.append(lax.ppermute(fresh_rows[:, 0], ("section", "tensor"), pairs))

    narrow = like((width, tokens), jnp.bfloat16)
    wide = like((width, tokens), jnp.float32)
    lanes = like((width, 128), jnp.bfloat16)
    turned = like((width, head_cols), jnp.bfloat16)
    product_flops = 2 * width * width * tokens
    norm_flops = 12 * width * tokens
    block_flops = 6 * product_flops

    scale, gate, own, other, hidden = call(
        first_kernel, [lanes, lanes, narrow, narrow, narrow], [SMEM] * 3 + [VMEM] * 3, 4 * norm_flops,
        (where, plan, timesteps, mod_own, mod_other, inflow[0]), "first",
    )

    def product(value):
        return call(
            product_kernel, [wide, narrow], [SMEM] + [VMEM] * 3, product_flops,
            (where, value, lin_own, lin_other), "product",
        )

    def joined(value, products, skip, tick, order):
        return call(
            functools.partial(joined_kernel, tick), [narrow, wide], [SMEM] + [VMEM] * 4 + [ANY], norm_flops,
            (where, value, products, skip, scale, order), "joined",
        )

    def attention(own, other, hidden, outs, tick, stage):
        results, scratch = [narrow], []
        if stage == "first":
            results = [narrow, turned, turned]
        if stage == "last":
            results = [like((half, tokens), jnp.float32)] * 2
            scratch = [pltpu.VMEM((width, tokens), jnp.float32)]
        return call(
            functools.partial(block_kernel, tick, stage), results, [SMEM] + [VMEM] * 8, block_flops,
            (where, own, other, hidden, gate, qkv_own, qkv_other, *outs), "attention_" + stage, scratch,
        )

    if middle <= sections - TICKS:
        products, outgoing = product(hidden)
        skip = moved(outgoing, [(low, sections - 1 - low) for low in range(middle)], "mirror0")
        own, hidden = joined(hidden, products, skip, 0, skip)
        other = swapped(own, "swap0")
    settled, *outs = attention(own, other, hidden, (out_own, out_other), 0, "first")

    arrived = moved(settled, [(low, low + 1) for low in range(sections - 2)], "relay0")
    fresh = call(
        fresh_kernel, [like((TICKS - 1, width, tokens), jnp.bfloat16)], [SMEM] + [VMEM] * len(blocks),
        norm_flops, (where, *blocks), "fresh",
    )[0]
    current, own = call(
        functools.partial(norm_kernel, 1), [narrow, narrow], [SMEM] + [VMEM] * 3, norm_flops,
        (where, arrived, fresh, scale), "norm",
    )
    other = swapped(own, "swap1")
    products, outgoing = product(current)
    skip = moved(outgoing, [(low, sections - 1 - low) for low in range(1, middle)], "mirror1")
    down = attention(own, other, current, outs, 1, "middle")[0]
    arrived_low = moved(down, [(low, low + 1) for low in range(middle)], "relay1_low")
    own, hidden = joined(current, products, skip, 1, down)
    other = swapped(own, "swap2")
    up = attention(own, other, hidden, outs, 1, "middle")[0]

    arrived = moved(up, [(low, low + 1) for low in range(middle, sections - 1)], "relay1_high")
    current, outgoing = call(
        functools.partial(skip_kernel, 2), [narrow, narrow], [SMEM] + [VMEM] * 4 + [ANY], product_flops,
        (where, arrived_low, fresh, lin_own, lin_other, up), "skip",
    )
    skip = moved(outgoing, [(low, sections - 1 - low) for low in range(middle)], "mirror2")
    received = jnp.where(section == middle, current, arrived)
    products, _ = product(received)
    own, hidden = joined(current, products, skip, 2, skip)
    other = swapped(own, "swap3")
    kept, sent = attention(own, other, hidden, outs, 2, "last")
    received = swapped(sent, "swap_out_columns")
    columns = jnp.where(
        core == 0,
        jnp.concatenate([kept, received], axis=1),
        jnp.concatenate([received, kept], axis=1),
    )
    return jnp.transpose(columns, (1, 0))[None]


def solution(mesh):
    return jax.shard_map(
        on_device,
        mesh=mesh,
        in_specs=(
            P("section", ("groups", "replica"), None),
            P(None, ("groups", "replica"), "section", None),
            P("section", None, "tensor"),
            P("section", None, None, "tensor"),
            P("section", "tensor", None),
            P("section", None, None, "tensor"),
            P(None, "section"),
            P(None, ("groups", "replica")),
        ),
        out_specs=P("section", ("groups", "replica"), "tensor"),
        check_vma=False,
    )
```

```python
import functools
import math

import jax
import jax.numpy as jnp
from jax import lax
from jax.experimental import pallas as pl
from jax.experimental.pallas import tpu as pltpu
from jax.sharding import PartitionSpec as P


DH = 72
FREQ = 128
TICKS = 3
EPSILON = 1e-06


VMEM = pl.BlockSpec(memory_space=pltpu.VMEM)
SMEM = pl.BlockSpec(memory_space=pltpu.SMEM)
ANY = pl.BlockSpec(memory_space=pl.ANY)
HBM = pl.BlockSpec(memory_space=pltpu.HBM)
TICK_LANES = 32
CHUNK = 96
PLACES = 3
FULL = 24 << 20


def call(body, outs, in_specs, flops, args, scratch=(), limit=24 << 20):
    moved = sum(math.prod(a.shape) * a.dtype.itemsize for a in (*args, *outs))
    return pl.pallas_call(
        body,
        out_shape=tuple(outs),
        in_specs=in_specs,
        out_specs=tuple(VMEM for _ in outs),
        scratch_shapes=list(scratch),
        compiler_params=pltpu.CompilerParams(vmem_limit_bytes=limit),
        cost_estimate=pl.CostEstimate(flops=flops, bytes_accessed=moved, transcendentals=0),
    )(*args)


def like(shape, dtype):
    return jax.ShapeDtypeStruct(shape, dtype)


def halves(tensor_index, half):
    own = pl.ds(pl.multiple_of(tensor_index * half, 16), half)
    other = pl.ds(pl.multiple_of((1 - tensor_index) * half, 16), half)
    return own, other


def column(ref, tick, rows=slice(None)):
    lane = tick * TICK_LANES
    return ref[rows, lane : lane + 1].astype(jnp.float32)


def folded(value):
    return jnp.sum(value.reshape(-1, 8, value.shape[-1]), axis=0)


def normalise(load, store, scale_ref, tick):
    count = scale_ref.shape[0]
    chunks = [slice(start, start + CHUNK) for start in range(0, count, CHUNK)]
    total = None
    for rows in chunks:
        part = folded(load(rows))
        total = part if total is None else total + part
    mean = jnp.sum(total, axis=0, keepdims=True) * (1.0 / count)
    total = None
    for rows in chunks:
        centred = load(rows) - mean
        part = folded(centred * centred)
        total = part if total is None else total + part
    variance = jnp.sum(total, axis=0, keepdims=True) * (1.0 / count)
    inverse = lax.rsqrt(variance + EPSILON)
    for rows in chunks:
        normed = (load(rows) - mean) * inverse
        store(rows, (normed * (1.0 + column(scale_ref, tick, rows))).astype(jnp.bfloat16))


def storing(ref):
    def store(rows, value):
        ref[rows, :] = value

    return store


def first_kernel(
    where, mod_own_hbm, mod_other_hbm, x_hbm,
    scale_ref, gate_ref, own_ref, other_ref, hidden_ref,
    mod_own, mod_other, x_ref, turned, sems,
):
    copies = [
        pltpu.make_async_copy(source, target, sems.at[index])
        for index, (source, target) in enumerate(
            ((mod_own_hbm, mod_own), (mod_other_hbm, mod_other), (x_hbm, x_ref))
        )
    ]
    for copy in copies:
        copy.start()
    half_freq = FREQ // 2
    lanes = scale_ref.shape[1]
    position = lax.broadcasted_iota(jnp.int32, (half_freq, lanes), 0).astype(jnp.float32)
    lane = lax.broadcasted_iota(jnp.int32, (half_freq, lanes), 1)
    frequency = jnp.exp(-math.log(10000.0) * position / half_freq)
    stamp = jnp.zeros((half_freq, lanes), jnp.float32)
    for tick in range(TICKS):
        moment = where[PLACES + TICKS + where[PLACES + tick]].astype(jnp.float32)
        stamp = jnp.where(lane // TICK_LANES == tick, moment, stamp)
    phases = stamp * frequency
    rest = jnp.concatenate([jnp.cos(phases), jnp.sin(phases)], axis=0)
    parts = []
    for _ in range(3):
        part = rest.astype(jnp.bfloat16)
        parts.append(part)
        rest = rest - part.astype(jnp.float32)
    stacked = jnp.concatenate(parts, axis=0)
    for copy in copies:
        copy.wait()
    half = mod_own.shape[1]
    for ref, rows in zip((mod_own, mod_other), halves(where[0], half)):
        for kind, target in enumerate((scale_ref, gate_ref)):
            weight = jnp.concatenate([ref[kind]] * 3, axis=1)
            product = jnp.dot(weight, stacked, preferred_element_type=jnp.float32)
            target[rows, :] = product.astype(jnp.bfloat16)
    tokens = own_ref.shape[1]
    turned[...] = jnp.transpose(x_ref[...].astype(jnp.float32), (1, 0))
    for index in range(2):
        columns = slice(index * tokens, (index + 1) * tokens)

        @pl.when(where[0] == index)
        def _():
            normalise(lambda rows: turned[rows, columns], storing(own_ref), scale_ref, 0)
            hidden_ref[...] = turned[:, columns].astype(jnp.bfloat16)

        @pl.when(where[0] != index)
        def _():
            normalise(lambda rows: turned[rows, columns], storing(other_ref), scale_ref, 0)


def norm_kernel(tick, where, arrived_ref, scale_ref, order_ref, *refs):
    *blocks, current_ref, mixed_ref, later_ref = refs

    @pl.when(where[2] == 0)
    def _():
        for index, target in enumerate((current_ref, later_ref)):
            head = jnp.where(
                where[0] == 0, blocks[0][index].astype(jnp.float32), blocks[1][index].astype(jnp.float32)
            )
            rows = [head] + [ref[index].astype(jnp.float32) for ref in blocks[2:]]
            target[...] = jnp.transpose(jnp.concatenate(rows, axis=0), (1, 0)).astype(jnp.bfloat16)

    @pl.when(where[2] != 0)
    def _():
        current_ref[...] = arrived_ref[...]

    normalise(lambda rows: current_ref[rows, :].astype(jnp.float32), storing(mixed_ref), scale_ref, tick)


def product_kernel(where, x_ref, own_ref, other_ref, *results):
    half = own_ref.shape[0]
    for ref, rows in zip((own_ref, other_ref), halves(where[0], half)):
        product = jnp.dot(ref[...], x_ref[...], preferred_element_type=jnp.float32)
        for result in results:
            result[rows, :] = product.astype(result.dtype)


def lowest_kernel(where, x_ref, own_ref, other_ref, order_ref, narrow_ref):
    @pl.when(where[2] == 0)
    def _():
        product_kernel(where, x_ref, own_ref, other_ref, narrow_ref)


def skip_kernel(where, x_ref, own_ref, other_ref, order_ref, narrow_ref):
    product_kernel(where, x_ref, own_ref, other_ref, narrow_ref)


def chosen_kernel(middle, where, low_ref, high_ref, own_ref, other_ref, wide_ref):
    half = own_ref.shape[0]
    value = jnp.where(where[2] == middle, low_ref[...], high_ref[...])
    for ref, rows in zip((own_ref, other_ref), halves(where[0], half)):
        wide_ref[rows, :] = jnp.dot(ref[...], value, preferred_element_type=jnp.float32)


def joined_kernel(tick, where, product_ref, skip_ref, scale_ref, order_ref, mixed_ref, hidden_ref):
    for start in range(0, product_ref.shape[0], CHUNK):
        rows = slice(start, start + CHUNK)
        hidden_ref[rows, :] = product_ref[rows, :] + skip_ref[rows, :].astype(jnp.float32)
    normalise(lambda rows: hidden_ref[rows, :], storing(mixed_ref), scale_ref, tick)


def last_joined_kernel(
    tick, last, where, fresh_ref, low_ref, product_ref, skip_ref, low_skip_ref, scale_ref, mixed_ref, hidden_ref
):
    @pl.when((where[1] == 1) & (where[2] == last))
    def _():
        hidden_ref[...] = product_ref[...] + low_skip_ref[...].astype(jnp.float32)

    @pl.when((where[1] == 1) & (where[2] != last))
    def _():
        hidden_ref[...] = product_ref[...] + skip_ref[...].astype(jnp.float32)

    @pl.when((where[1] == 0) & (where[2] == 0))
    def _():
        hidden_ref[...] = fresh_ref[...].astype(jnp.float32)

    @pl.when((where[1] == 0) & (where[2] != 0))
    def _():
        hidden_ref[...] = low_ref[...].astype(jnp.float32)

    normalise(lambda rows: hidden_ref[rows, :], storing(mixed_ref), scale_ref, tick)


def block_kernel(
    tick, stage, where, own_ref, other_ref, hidden_ref, gate_ref, qkv_own, qkv_other, out_own, out_other, *rest
):
    if stage == "first":
        *results, scores, raised, attended, held_a, held_b, raw_a, raw_b, sems = rest
        copies = [
            pltpu.make_async_copy(source, target, sems.at[index])
            for index, (source, target) in enumerate(
                ((qkv_own, held_a), (qkv_other, held_b), (out_own, raw_a), (out_other, raw_b))
            )
        ]
        for copy in copies:
            copy.start()
        projections, turned = (held_a, held_b), results[1:]
    else:
        *results, scores, raised, attended = rest
        projections, turned = (qkv_own, qkv_other), (out_own, out_other)
    own = own_ref[...]
    both = jnp.concatenate([own, other_ref[...]], axis=1)
    head_cols = projections[0].shape[1]
    heads = head_cols // DH
    values = []
    for group, ref in enumerate(projections):
        if stage == "first":
            copies[group].wait()
        query = jnp.dot(ref[0], own, preferred_element_type=jnp.float32).astype(jnp.bfloat16)
        key = jnp.dot(ref[1], both, preferred_element_type=jnp.float32).astype(jnp.bfloat16)
        values.append(jnp.dot(ref[2], both, preferred_element_type=jnp.float32).astype(jnp.bfloat16))
        for head in range(heads):
            rows = slice(head * DH, (head + 1) * DH)
            scores[group * heads + head] = lax.dot_general(
                key[rows], query[rows], (((0,), (0,)), ((), ())), preferred_element_type=jnp.float32
            ) * (1.0 / math.sqrt(DH))
    if stage == "first":
        for index, (source, target) in enumerate(zip((raw_a, raw_b), turned)):
            copies[2 + index].wait()
            target[...] = jnp.transpose(source[...].astype(jnp.float32), (1, 0)).astype(jnp.bfloat16)
    weights = []
    for head in range(2 * heads):
        value = scores[head]
        power = jnp.exp(value - jnp.max(value, axis=0, keepdims=True))
        weights.append(jnp.sum(power, axis=0, keepdims=True))
        raised[head] = power.astype(jnp.bfloat16)
    total = None
    for group, out_ref in enumerate(turned):
        for head in range(heads):
            rows = slice(head * DH, (head + 1) * DH)
            place = group * heads + head
            attended[place * DH : (place + 1) * DH, :] = (
                jnp.dot(values[group][rows], raised[place], preferred_element_type=jnp.float32) / weights[place]
            )
        rows = slice(group * head_cols, (group + 1) * head_cols)
        term = jnp.dot(out_ref[...], attended[rows, :].astype(jnp.bfloat16), preferred_element_type=jnp.float32)
        term = term.astype(jnp.bfloat16).astype(jnp.float32)
        total = term if total is None else total + term
    result = hidden_ref[...].astype(jnp.float32) + column(gate_ref, tick) * total
    if stage == "last":
        kept_ref, sent_ref, full_ref = results
        full_ref[...] = result
        own_rows, other_rows = halves(where[0], kept_ref.shape[0])
        kept_ref[...] = full_ref[own_rows, :]
        sent_ref[...] = full_ref[other_rows, :]
    else:
        results[0][...] = result.astype(jnp.bfloat16)


def relayed(inflow, fresh_rows, lin_weight, qkv_weight, out_weight, mod_weight, plan, timesteps):
    sections = lax.axis_size("section")
    middle = sections // 2
    section = lax.axis_index("section")
    core = lax.axis_index("tensor")
    _, row_count, width = inflow.shape
    tokens = row_count // lax.axis_size("tensor")
    half = lin_weight.shape[2]
    head_cols = out_weight.shape[1]
    if lax.axis_size("tensor") != 2 or timesteps.shape[1] != 1 or sections < 4:
        raise ValueError("unsupported split")
    where = jnp.concatenate(
        [jnp.stack([core, (section >= middle).astype(jnp.int32), section]), plan[:, 0], timesteps[:, 0]]
    ).astype(jnp.int32)

    def swapped(value):
        return lax.ppermute(value, "tensor", [(0, 1), (1, 0)])

    def moved(value, pairs):
        return lax.ppermute(value, "section", pairs)

    mod_own = jnp.transpose(mod_weight[0], (1, 2, 0))
    qkv_own = jnp.transpose(qkv_weight[0], (0, 2, 1))
    lin_own = jnp.transpose(lin_weight[0], (1, 0))
    out_own = out_weight[0]
    mod_other = swapped(mod_own)
    qkv_other = swapped(qkv_own)
    out_other = swapped(out_own)

    narrow = like((width, tokens), jnp.bfloat16)
    wide = like((width, tokens), jnp.float32)
    lanes = like((width, 128), jnp.bfloat16)
    turned = like((width, head_cols), jnp.bfloat16)
    product_flops = 2 * width * width * tokens
    norm_flops = 12 * width * tokens
    block_flops = 6 * product_flops

    scale, gate, own, other, hidden = call(
        first_kernel, [lanes, lanes, narrow, narrow, narrow], [SMEM] + [HBM] * 3, 4 * norm_flops,
        (where, mod_own, mod_other, inflow[0]),
        [
            pltpu.VMEM(mod_own.shape, jnp.bfloat16),
            pltpu.VMEM(mod_own.shape, jnp.bfloat16),
            pltpu.VMEM((row_count, width), jnp.bfloat16),
            pltpu.VMEM((width, row_count), jnp.float32),
            pltpu.SemaphoreType.DMA((3,)),
        ],
        FULL,
    )

    def attention(own, other, hidden, outs, tick, stage):
        results = [narrow]
        count = 2 * head_cols // DH
        scratch = [
            pltpu.VMEM((count, row_count, tokens), jnp.float32),
            pltpu.VMEM((count, row_count, tokens), jnp.bfloat16),
            pltpu.VMEM((2 * head_cols, tokens), jnp.float32),
        ]
        weights = [VMEM] * 4
        if stage == "first":
            results = [narrow, turned, turned]
            weights = [HBM] * 4
            scratch += [pltpu.VMEM(qkv_own.shape, jnp.bfloat16)] * 2
            scratch += [pltpu.VMEM(out_own.shape, jnp.bfloat16)] * 2
            scratch += [pltpu.SemaphoreType.DMA((4,))]
        if stage == "last":
            results = [like((half, tokens), jnp.float32)] * 2
            scratch = [pltpu.VMEM((width, tokens), jnp.float32)] + scratch
        return call(
            functools.partial(block_kernel, tick, stage), results, [SMEM] + [VMEM] * 4 + weights, block_flops,
            (where, own, other, hidden, gate, qkv_own, qkv_other, *outs), scratch,
            FULL if stage == "first" else 24 << 20,
        )

    early = middle <= sections - TICKS
    if early:
        lin_other = swapped(lin_own)
        products, outgoing = call(
            product_kernel, [wide, narrow], [SMEM] + [VMEM] * 3, product_flops,
            (where, hidden, lin_own, lin_other),
        )
        skip = moved(outgoing, [(low, sections - 1 - low) for low in range(middle)])
        mixed, joined = call(
            functools.partial(joined_kernel, 0), [narrow, wide], [SMEM] + [VMEM] * 3 + [ANY], norm_flops,
            (where, products, skip, scale, skip),
        )
        upper = section >= middle
        own = jnp.where(upper, mixed, own)
        hidden = jnp.where(upper, joined, hidden.astype(jnp.float32))
        other = swapped(own)
    settled, *outs = attention(own, other, hidden, (out_own, out_other), 0, "first")

    arrived = moved(settled, [(low, low + 1) for low in range(sections - 2)])
    fresh_block, lin_source, _ = lax.optimization_barrier((fresh_rows[:, 0], lin_own, settled))
    if not early:
        lin_other = swapped(lin_source)
    blocks = [fresh_block]
    for place in range(middle):
        pairs = [
            ((side * middle + place) * 2 + side, side) for side in range(2) if side or place
        ]
        blocks.append(lax.ppermute(fresh_block, ("section", "tensor"), pairs))
    products, outgoing = call(
        product_kernel, [wide, narrow], [SMEM] + [VMEM] * 3, product_flops,
        (where, arrived, lin_own, lin_other),
    )
    skip = moved(outgoing, [(low, sections - 1 - low) for low in range(1, middle)])
    current, own, later = call(
        functools.partial(norm_kernel, 1), [narrow] * 3, [SMEM] + [VMEM] * 2 + [ANY] + [VMEM] * len(blocks), norm_flops,
        (where, arrived, scale, outgoing, *blocks),
    )
    other = swapped(own)
    down = attention(own, other, current, outs, 1, "middle")[0]
    arrived_low = moved(down, [(low, low + 1) for low in range(middle)])
    lowest = call(
        lowest_kernel, [narrow], [SMEM] + [VMEM] * 3 + [ANY], product_flops,
        (where, later, lin_own, lin_other, down),
    )[0]
    low_skip = moved(lowest, [(0, sections - 1)])
    own, hidden = call(
        functools.partial(joined_kernel, 1), [narrow, wide], [SMEM] + [VMEM] * 3 + [ANY], norm_flops,
        (where, products, skip, scale, lowest),
    )
    other = swapped(own)
    up = attention(own, other, hidden, outs, 1, "middle")[0]

    arrived_high = moved(up, [(low, low + 1) for low in range(middle, sections - 1)])
    outgoing = call(
        skip_kernel, [narrow], [SMEM] + [VMEM] * 3 + [ANY], product_flops,
        (where, arrived_low, lin_own, lin_other, up),
    )[0]
    skip = moved(outgoing, [(low, sections - 1 - low) for low in range(1, middle)])
    products = call(
        functools.partial(chosen_kernel, middle), [wide], [SMEM] + [VMEM] * 4, product_flops,
        (where, arrived_low, arrived_high, lin_own, lin_other),
    )[0]
    own, hidden = call(
        functools.partial(last_joined_kernel, 2, sections - 1), [narrow, wide], [SMEM] + [VMEM] * 6, norm_flops,
        (where, later, arrived_low, products, skip, low_skip, scale),
    )
    other = swapped(own)
    kept, sent = attention(own, other, hidden, outs, 2, "last")
    received = swapped(sent)
    columns = jnp.where(
        core == 0,
        jnp.concatenate([kept, received], axis=1),
        jnp.concatenate([received, kept], axis=1),
    )
    return jnp.transpose(columns, (1, 0))[None]


def solution(mesh):
    return jax.shard_map(
        relayed,
        mesh=mesh,
        in_specs=(
            P("section", ("groups", "replica"), None),
            P(None, ("groups", "replica"), "section", None),
            P("section", None, "tensor"),
            P("section", None, None, "tensor"),
            P("section", "tensor", None),
            P("section", None, None, "tensor"),
            P(None, "section"),
            P(None, ("groups", "replica")),
        ),
        out_specs=P("section", ("groups", "replica"), "tensor"),
        check_vma=False,
    )
```

```python
import functools
import math

import jax
import jax.numpy as jnp
from jax import lax
from jax.experimental import pallas as pl
from jax.experimental.pallas import tpu as pltpu
from jax.sharding import PartitionSpec as P


DH = 72
FREQ = 128
TICKS = 3
EPSILON = 1e-06


VMEM = pl.BlockSpec(memory_space=pltpu.VMEM)
SMEM = pl.BlockSpec(memory_space=pltpu.SMEM)
ANY = pl.BlockSpec(memory_space=pl.ANY)
HBM = pl.BlockSpec(memory_space=pltpu.HBM)
TICK_LANES = 32
CHUNK = 96
PLACES = 3


def call(body, outs, in_specs, flops, args, scratch=()):
    moved = sum(math.prod(a.shape) * a.dtype.itemsize for a in (*args, *outs))
    args = [
        pltpu.with_memory_space_constraint(a, pltpu.HBM) if spec is HBM else a for a, spec in zip(args, in_specs)
    ]
    return pl.pallas_call(
        body,
        out_shape=tuple(outs),
        in_specs=in_specs,
        out_specs=tuple(VMEM for _ in outs),
        scratch_shapes=list(scratch),
        compiler_params=pltpu.CompilerParams(vmem_limit_bytes=24 << 20),
        cost_estimate=pl.CostEstimate(flops=flops, bytes_accessed=moved, transcendentals=0),
    )(*args)


def like(shape, dtype):
    return jax.ShapeDtypeStruct(shape, dtype)


def halves(tensor_index, half):
    own = pl.ds(pl.multiple_of(tensor_index * half, 16), half)
    other = pl.ds(pl.multiple_of((1 - tensor_index) * half, 16), half)
    return own, other


def column(ref, tick, rows=slice(None)):
    lane = tick * TICK_LANES
    return ref[rows, lane : lane + 1].astype(jnp.float32)


def folded(value):
    return jnp.sum(value.reshape(-1, 8, value.shape[-1]), axis=0)


def normalise(load, store, scale_ref, tick):
    count = scale_ref.shape[0]
    chunks = [slice(start, start + CHUNK) for start in range(0, count, CHUNK)]
    total = None
    for rows in chunks:
        part = folded(load(rows))
        total = part if total is None else total + part
    mean = jnp.sum(total, axis=0, keepdims=True) * (1.0 / count)
    total = None
    for rows in chunks:
        centred = load(rows) - mean
        part = folded(centred * centred)
        total = part if total is None else total + part
    variance = jnp.sum(total, axis=0, keepdims=True) * (1.0 / count)
    inverse = lax.rsqrt(variance + EPSILON)
    for rows in chunks:
        normed = (load(rows) - mean) * inverse
        store(rows, (normed * (1.0 + column(scale_ref, tick, rows))).astype(jnp.bfloat16))


def storing(ref):
    def store(rows, value):
        ref[rows, :] = value

    return store


def first_kernel(
    where, mod_own_hbm, x_hbm, mod_other,
    scale_ref, gate_ref, own_ref, other_ref, hidden_ref,
    mod_own, x_ref, turned, sems,
):
    copies = [
        pltpu.make_async_copy(source, target, sems.at[index])
        for index, (source, target) in enumerate(
            ((mod_own_hbm, mod_own), (x_hbm, x_ref))
        )
    ]
    for copy in copies:
        copy.start()
    half_freq = FREQ // 2
    lanes = scale_ref.shape[1]
    position = lax.broadcasted_iota(jnp.int32, (half_freq, lanes), 0).astype(jnp.float32)
    lane = lax.broadcasted_iota(jnp.int32, (half_freq, lanes), 1)
    frequency = jnp.exp(-math.log(10000.0) * position / half_freq)
    stamp = jnp.zeros((half_freq, lanes), jnp.float32)
    for tick in range(TICKS):
        moment = where[PLACES + TICKS + where[PLACES + tick]].astype(jnp.float32)
        stamp = jnp.where(lane // TICK_LANES == tick, moment, stamp)
    phases = stamp * frequency
    rest = jnp.concatenate([jnp.cos(phases), jnp.sin(phases)], axis=0)
    parts = []
    for _ in range(3):
        part = rest.astype(jnp.bfloat16)
        parts.append(part)
        rest = rest - part.astype(jnp.float32)
    stacked = jnp.concatenate(parts, axis=0)
    for copy in copies:
        copy.wait()
    half = mod_own.shape[1]
    for ref, rows in zip((mod_own, mod_other), halves(where[0], half)):
        for kind, target in enumerate((scale_ref, gate_ref)):
            weight = jnp.concatenate([ref[kind]] * 3, axis=1)
            product = jnp.dot(weight, stacked, preferred_element_type=jnp.float32)
            target[rows, :] = product.astype(jnp.bfloat16)
    tokens = own_ref.shape[1]
    turned[...] = jnp.transpose(x_ref[...].astype(jnp.float32), (1, 0))
    for index in range(2):
        columns = slice(index * tokens, (index + 1) * tokens)

        @pl.when(where[0] == index)
        def _():
            normalise(lambda rows: turned[rows, columns], storing(own_ref), scale_ref, 0)
            hidden_ref[...] = turned[:, columns].astype(jnp.bfloat16)

        @pl.when(where[0] != index)
        def _():
            normalise(lambda rows: turned[rows, columns], storing(other_ref), scale_ref, 0)


def ahead_norm_kernel(tick, where, scale_ref, *refs):
    *blocks, current_ref, mixed_ref, later_ref = refs

    @pl.when(where[2] == 0)
    def _():
        for index, target in enumerate((current_ref, later_ref)):
            head = jnp.where(
                where[0] == 0, blocks[0][index].astype(jnp.float32), blocks[1][index].astype(jnp.float32)
            )
            rows = [head] + [ref[index].astype(jnp.float32) for ref in blocks[2:]]
            target[...] = jnp.transpose(jnp.concatenate(rows, axis=0), (1, 0)).astype(jnp.bfloat16)
        normalise(lambda rows: current_ref[rows, :].astype(jnp.float32), storing(mixed_ref), scale_ref, tick)


def norm_kernel(tick, where, x_ref, scale_ref, order_ref, mixed_ref):
    normalise(lambda rows: x_ref[rows, :].astype(jnp.float32), storing(mixed_ref), scale_ref, tick)


def multiply(where, value, own_ref, other_ref, results):
    for ref, rows in zip((own_ref, other_ref), halves(where[0], own_ref.shape[0])):
        product = jnp.dot(ref[...], value, preferred_element_type=jnp.float32)
        for result in results:
            result[rows, :] = product.astype(result.dtype)


def product_kernel(where, x_ref, own_ref, other_ref, *results):
    multiply(where, x_ref[...], own_ref, other_ref, results)


def outgoing_kernel(where, x_ref, ahead_ref, own_ref, other_ref, order_ref, wide_ref, narrow_ref):
    @pl.when(where[2] == 0)
    def _():
        narrow_ref[...] = ahead_ref[...]

    @pl.when(where[2] != 0)
    def _():
        multiply(where, x_ref[...], own_ref, other_ref, (wide_ref, narrow_ref))


def lowest_kernel(where, x_ref, own_ref, other_ref, order_ref, narrow_ref):
    @pl.when(where[2] == 0)
    def _():
        multiply(where, x_ref[...], own_ref, other_ref, (narrow_ref,))


def skip_kernel(where, low_ref, ahead_ref, own_ref, other_ref, order_ref, narrow_ref):
    @pl.when(where[2] == 1)
    def _():
        multiply(where, ahead_ref[...], own_ref, other_ref, (narrow_ref,))

    @pl.when((where[1] == 0) & (where[2] > 1))
    def _():
        multiply(where, low_ref[...], own_ref, other_ref, (narrow_ref,))


def joined_kernel(tick, where, product_ref, skip_ref, scale_ref, order_ref, mixed_ref, hidden_ref):
    for start in range(0, product_ref.shape[0], CHUNK):
        rows = slice(start, start + CHUNK)
        hidden_ref[rows, :] = product_ref[rows, :] + skip_ref[rows, :].astype(jnp.float32)
    normalise(lambda rows: hidden_ref[rows, :], storing(mixed_ref), scale_ref, tick)


def last_joined_kernel(
    tick, middle, last, where, fresh_ref, ahead_ref, low_ref, high_ref, skip_ref, low_skip_ref, own_ref, other_ref,
    scale_ref, mixed_ref, hidden_ref,
):
    @pl.when(where[1] == 1)
    def _():
        value = jnp.where(where[2] == middle, low_ref[...], high_ref[...])
        multiply(where, value, own_ref, other_ref, (hidden_ref,))

    for here, source in (
        (where[2] == 0, fresh_ref),
        (where[2] == 1, ahead_ref),
        ((where[1] == 0) & (where[2] > 1), low_ref),
    ):

        @pl.when(here)
        def _():
            hidden_ref[...] = source[...].astype(jnp.float32)

    for here, source in (
        ((where[1] == 1) & (where[2] == last), low_skip_ref),
        ((where[1] == 1) & (where[2] != last), skip_ref),
    ):

        @pl.when(here)
        def _():
            hidden_ref[...] += source[...].astype(jnp.float32)

    normalise(lambda rows: hidden_ref[rows, :], storing(mixed_ref), scale_ref, tick)


def ahead_block_kernel(tick, where, *refs):
    @pl.when(where[2] == 0)
    def _():
        block_kernel(tick, "middle", where, *refs)


def block_kernel(
    tick, stage, where, order_ref, own_ref, other_ref, hidden_ref, gate_ref, qkv_own, qkv_other, out_own, out_other,
    *rest,
):
    if stage == "first":
        *results, scores, raised, attended, held, raw, sems = rest
        copies = [
            pltpu.make_async_copy(source, target, sems.at[index])
            for index, (source, target) in enumerate(((qkv_own, held), (out_own, raw)))
        ]
        for copy in copies:
            copy.start()
        projections, turned = (qkv_other, held), results[2:0:-1]
    else:
        *results, scores, raised, attended = rest
        projections, turned = (qkv_own, qkv_other), (out_own, out_other)
    own = own_ref[...]
    both = jnp.concatenate([own, other_ref[...]], axis=1)
    head_cols = projections[0].shape[1]
    heads = head_cols // DH
    values = []
    for group, ref in enumerate(projections):
        if stage == "first" and group == 1:
            copies[0].wait()
        query = jnp.dot(ref[0], own, preferred_element_type=jnp.float32).astype(jnp.bfloat16)
        key = jnp.dot(ref[1], both, preferred_element_type=jnp.float32).astype(jnp.bfloat16)
        values.append(jnp.dot(ref[2], both, preferred_element_type=jnp.float32).astype(jnp.bfloat16))
        for head in range(heads):
            rows = slice(head * DH, (head + 1) * DH)
            scores[group * heads + head] = lax.dot_general(
                key[rows], query[rows], (((0,), (0,)), ((), ())), preferred_element_type=jnp.float32
            ) * (1.0 / math.sqrt(DH))
    if stage == "first":
        copies[1].wait()
        for source, target in zip((out_other, raw), turned):
            target[...] = jnp.transpose(source[...].astype(jnp.float32), (1, 0)).astype(jnp.bfloat16)
    weights = []
    for head in range(2 * heads):
        value = scores[head]
        power = jnp.exp(value - jnp.max(value, axis=0, keepdims=True))
        weights.append(jnp.sum(power, axis=0, keepdims=True))
        raised[head] = power.astype(jnp.bfloat16)
    total = None
    for group, out_ref in enumerate(turned):
        for head in range(heads):
            rows = slice(head * DH, (head + 1) * DH)
            place = group * heads + head
            attended[place * DH : (place + 1) * DH, :] = (
                jnp.dot(values[group][rows], raised[place], preferred_element_type=jnp.float32) / weights[place]
            )
        rows = slice(group * head_cols, (group + 1) * head_cols)
        term = jnp.dot(out_ref[...], attended[rows, :].astype(jnp.bfloat16), preferred_element_type=jnp.float32)
        term = term.astype(jnp.bfloat16).astype(jnp.float32)
        total = term if total is None else total + term
    result = hidden_ref[...].astype(jnp.float32) + column(gate_ref, tick) * total
    if stage == "last":
        kept_ref, sent_ref, full_ref = results
        full_ref[...] = result
        own_rows, other_rows = halves(where[0], kept_ref.shape[0])
        kept_ref[...] = full_ref[own_rows, :]
        sent_ref[...] = full_ref[other_rows, :]
    else:
        results[0][...] = result.astype(jnp.bfloat16)


def relayed(inflow, fresh_rows, lin_weight, qkv_weight, out_weight, mod_weight, plan, timesteps):
    sections = lax.axis_size("section")
    middle = sections // 2
    section = lax.axis_index("section")
    core = lax.axis_index("tensor")
    _, row_count, width = inflow.shape
    tokens = row_count // lax.axis_size("tensor")
    half = lin_weight.shape[2]
    head_cols = out_weight.shape[1]
    if lax.axis_size("tensor") != 2 or timesteps.shape[1] != 1 or sections < 4:
        raise ValueError("unsupported split")
    where = jnp.concatenate(
        [jnp.stack([core, (section >= middle).astype(jnp.int32), section]), plan[:, 0], timesteps[:, 0]]
    ).astype(jnp.int32)

    def swapped(value):
        return lax.ppermute(value, "tensor", [(0, 1), (1, 0)])

    def moved(value, pairs):
        return lax.ppermute(value, "section", pairs)

    mod_own = jnp.transpose(mod_weight[0], (1, 2, 0))
    qkv_own = jnp.transpose(qkv_weight[0], (0, 2, 1))
    lin_own = jnp.transpose(lin_weight[0], (1, 0))
    out_own = out_weight[0]
    mod_other = swapped(mod_own)
    qkv_other = swapped(qkv_own)
    out_other = swapped(out_own)

    narrow = like((width, tokens), jnp.bfloat16)
    wide = like((width, tokens), jnp.float32)
    lanes = like((width, 128), jnp.bfloat16)
    turned = like((width, head_cols), jnp.bfloat16)
    product_flops = 2 * width * width * tokens
    norm_flops = 12 * width * tokens
    block_flops = 6 * product_flops

    scale, gate, own, other, hidden = call(
        first_kernel, [lanes, lanes, narrow, narrow, narrow], [SMEM, HBM, HBM, VMEM], 4 * norm_flops,
        (where, mod_own, inflow[0], mod_other),
        [
            pltpu.VMEM(mod_own.shape, jnp.bfloat16),
            pltpu.VMEM((row_count, width), jnp.bfloat16),
            pltpu.VMEM((width, row_count), jnp.float32),
            pltpu.SemaphoreType.DMA((2,)),
        ],
    )

    def attention(own, other, hidden, outs, tick, stage, order):
        results = [narrow]
        count = 2 * head_cols // DH
        scratch = [
            pltpu.VMEM((count, row_count, tokens), jnp.float32),
            pltpu.VMEM((count, row_count, tokens), jnp.bfloat16),
            pltpu.VMEM((2 * head_cols, tokens), jnp.float32),
        ]
        weights = [VMEM] * 4
        if stage == "first":
            results = [narrow, turned, turned]
            weights = [HBM, VMEM, HBM, VMEM]
            scratch += [pltpu.VMEM(qkv_own.shape, jnp.bfloat16), pltpu.VMEM(out_own.shape, jnp.bfloat16)]
            scratch += [pltpu.SemaphoreType.DMA((2,))]
        if stage == "last":
            results = [like((half, tokens), jnp.float32)] * 2
            scratch = [pltpu.VMEM((width, tokens), jnp.float32)] + scratch
        return call(
            functools.partial(ahead_block_kernel, tick) if stage == "ahead" else functools.partial(block_kernel, tick, stage),
            results, [SMEM, ANY] + [VMEM] * 4 + weights, block_flops,
            (where, order, own, other, hidden, gate, qkv_own, qkv_other, *outs), scratch,
        )

    blocks = [fresh_rows[:, 0]]
    for place in range(middle):
        pairs = [
            ((side * middle + place) * 2 + side, side) for side in range(2) if side or place
        ]
        blocks.append(lax.ppermute(fresh_rows[:, 0], ("section", "tensor"), pairs))

    early = middle <= sections - TICKS
    if early:
        lin_other = swapped(lin_own)
        products, outgoing = call(
            product_kernel, [wide, narrow], [SMEM] + [VMEM] * 3, product_flops,
            (where, hidden, lin_own, lin_other),
        )
        skip = moved(outgoing, [(low, sections - 1 - low) for low in range(middle)])
        mixed, joined = call(
            functools.partial(joined_kernel, 0), [narrow, wide], [SMEM] + [VMEM] * 3 + [ANY], norm_flops,
            (where, products, skip, scale, skip),
        )
        upper = section >= middle
        own = jnp.where(upper, mixed, own)
        hidden = jnp.where(upper, joined, hidden.astype(jnp.float32))
        other = swapped(own)
    settled, *outs = attention(own, other, hidden, (out_own, out_other), 0, "first", own)
    arrived = moved(settled, [(low, low + 1) for low in range(sections - 2)])
    if not early:
        lin_source, _ = lax.optimization_barrier((lin_own, settled))
        lin_other = swapped(lin_source)

    current, own, later = call(
        functools.partial(ahead_norm_kernel, 1), [narrow] * 3, [SMEM] + [VMEM] * (1 + len(blocks)), norm_flops,
        (where, scale, *blocks),
    )
    other = swapped(own)
    ahead = attention(own, other, current, outs, 1, "ahead", own)[0]
    lowest = call(
        lowest_kernel, [narrow], [SMEM] + [VMEM] * 3 + [ANY], product_flops,
        (where, later, lin_own, lin_other, ahead),
    )[0]
    low_skip = moved(lowest, [(0, sections - 1)])

    products, outgoing = call(
        outgoing_kernel, [wide, narrow], [SMEM] + [VMEM] * 4 + [ANY], product_flops,
        (where, arrived, ahead, lin_own, lin_other, lowest),
    )
    skip = moved(outgoing, [(0, 1)] + [(low, sections - 1 - low) for low in range(1, middle)])
    own = call(
        functools.partial(norm_kernel, 1), [narrow], [SMEM] + [VMEM] * 2 + [ANY], norm_flops,
        (where, arrived, scale, outgoing),
    )[0]
    other = swapped(own)
    down = attention(own, other, arrived, outs, 1, "middle", own)[0]
    arrived_low = moved(down, [(low, low + 1) for low in range(1, middle)])
    ahead = skip
    own, hidden = call(
        functools.partial(joined_kernel, 1), [narrow, wide], [SMEM] + [VMEM] * 3 + [ANY], norm_flops,
        (where, products, skip, scale, down),
    )
    other = swapped(own)
    outgoing = call(
        skip_kernel, [narrow], [SMEM] + [VMEM] * 4 + [ANY], product_flops,
        (where, arrived_low if middle > 2 else ahead, ahead, lin_own, lin_other, own),
    )[0]
    skip = moved(outgoing, [(low, sections - 1 - low) for low in range(1, middle)])
    up = attention(own, other, hidden, outs, 1, "middle", outgoing)[0]

    arrived_high = moved(up, [(low, low + 1) for low in range(middle, sections - 1)])
    own, hidden = call(
        functools.partial(last_joined_kernel, 2, middle, sections - 1), [narrow, wide],
        [SMEM] + [VMEM] * 9, product_flops,
        (where, later, ahead, arrived_low, arrived_high, skip, low_skip, lin_own, lin_other, scale),
    )
    other = swapped(own)
    kept, sent = attention(own, other, hidden, outs, 2, "last", own)
    received = swapped(sent)
    columns = jnp.where(
        core == 0,
        jnp.concatenate([kept, received], axis=1),
        jnp.concatenate([received, kept], axis=1),
    )
    return jnp.transpose(columns, (1, 0))[None]


def solution(mesh):
    return jax.shard_map(
        relayed,
        mesh=mesh,
        in_specs=(
            P("section", ("groups", "replica"), None),
            P(None, ("groups", "replica"), "section", None),
            P("section", None, "tensor"),
            P("section", None, None, "tensor"),
            P("section", "tensor", None),
            P("section", None, None, "tensor"),
            P(None, "section"),
            P(None, ("groups", "replica")),
        ),
        out_specs=P("section", ("groups", "replica"), "tensor"),
        check_vma=False,
    )
```
